1024 devices in a mesh: section: 16 (over x, y), seq: 64 (over z, core).
Axes of the slice: x: 4, y: 4, z: 32, core: 2. Of those that a mesh axis runs over, the one named last changes fastest.
Arguments:
- grad_out: bfloat16 [16, 4096, 8192], P('section', 'seq'), may hold values from -6 to 6
- step_sizes: float32 [16, 128, 8192], P('section', None, 'seq'), may hold values from 0.01 to 0.1
- decay_rate: float32 [16, 128], P('section', 'seq'), may hold values from 0.001 to 1
- skip_gain: float32 [16, 128], P('section', 'seq'), may hold values from 0.5 to 1.5
- state_in: bfloat16 [16, 8, 8192, 128], P('section', None, 'seq'), may hold values from -6 to 6
- state_out: bfloat16 [16, 8, 8192, 128], P('section', None, 'seq'), may hold values from -0.5 to 0.5
- segment_ids: int32 [16, 8192], P('section'), may hold values from 0 to 15, never falling along the last dimension, each value on 1 to 4096 neighbouring positions
Outputs:
- incoming: bfloat16 [16, 4096, 8192], P('section', 'seq')
The draws below stay inside these ranges and needn't reach their ends.
All inputs are finite; a program needn't handle non-finite values.
Results may differ from the reference program's by a relative error of at most 0.007.
Values may be sent and summed in bfloat16 or wider, within the bound.
No kernel may reach another device: no remote copies, remote signals or barrier semaphores. Data moves between devices by JAX's collectives and lax.ppermute only.
A program may use at most 32 MiB of HBM per device.

```python
import math
import jax
import jax.numpy as jnp
import numpy as np
from jax import lax

SEQLEN = 8192
SECTIONS = 16
HEADS = 128
HEAD_DIM = 32
STATE = 128
GROUPS = 8
SPAN = 256
DOCS = 16


def block_scale(own_key, shape, pieces, smallest, high):
    loudness, own = 1.0, jax.random.fold_in(own_key, 6)
    for dim, blocks in pieces:
        draws = jnp.exp(jax.random.uniform(jax.random.fold_in(own, dim), (blocks,), jnp.float32, smallest / len(pieces), high / len(pieces)))
        loudness = loudness * jnp.repeat(draws, shape[dim] // blocks).reshape([-1 if axis == dim else 1 for axis in range(len(shape))])
    return loudness


def profile(number_of, total, reach, skew):
    portions = [(1 << 20) // math.isqrt(rank ** skew) + 1 for rank in range(2, number_of + 1)]
    rest, holding = total - reach - (number_of - 1), [1] * (number_of - 1)
    while rest > 0:
        candidates = [i for i in range(number_of - 1) if holding[i] < reach]
        whole, remaining = sum([portions[i] for i in candidates]), rest
        for i in candidates:
            addition = min(reach - holding[i], max(1, remaining * portions[i] // whole), rest)
            holding[i] = holding[i] + addition
            rest = rest - addition
    return np.array([reach] + holding)


def uneven(rng, amount, total, limit, slope):
    if amount == 2:
        one = jax.random.randint(rng, (), max(1, total - limit), min(limit, total - 1) + 1)
        return jnp.stack([one, total - one])
    tallies = jnp.asarray(profile(amount, total, limit, slope), jnp.int32)
    twos = (amount - 1) // 2
    donor, taker = tallies[1:1 + 2 * twos:2], tallies[2:2 + 2 * twos:2]
    room = jnp.minimum(donor - 1, limit - taker)
    shifted = jax.random.randint(jax.random.fold_in(rng, 1), (twos,), 0, 1 << 20) % (room + 1)
    tallies = tallies.at[1:1 + 2 * twos:2].set(donor - shifted).at[2:2 + 2 * twos:2].set(taker + shifted)
    return tallies[jax.random.permutation(jax.random.fold_in(rng, 2), amount)]


def normal_values(own_key, extent, scale, bound, shards=(), held_as=jnp.bfloat16):
    factor_of = block_scale(own_key, extent, shards, -0.22, 0.18) if shards else 1.0
    array = jax.random.normal(own_key, extent, jnp.float32) * scale * factor_of
    return jnp.minimum(jnp.maximum(array, -bound), bound).astype(held_as)


def setup_inputs(seed: int = 0) -> dict:
    key_of = jax.random.split(jax.random.key(seed), 8)
    grad_out = normal_values(key_of[0], (SECTIONS, HEADS * HEAD_DIM, SEQLEN), 1.0, 6.0, ((0, 16), (1, 64)))
    step_sizes = jnp.clip(jnp.exp(math.log(0.1) - 2.3025851 * jax.random.uniform(key_of[1], (SECTIONS, HEADS, SEQLEN), jnp.float32) ** block_scale(key_of[1], (SECTIONS, HEADS, SEQLEN), ((0, 16), (2, 64)), -0.2, 0.2)), 0.01, 0.1)
    decay_rate = jnp.clip(jnp.exp(math.log(1.0) - 6.9077552 * jax.random.uniform(key_of[2], (SECTIONS, HEADS), jnp.float32) ** block_scale(key_of[2], (SECTIONS, HEADS), ((0, 16), (1, 64)), -0.2, 0.2)), 0.001, 1.0)
    skip_gain = jnp.clip(0.5 + 1.0 * jax.random.uniform(key_of[3], (SECTIONS, HEADS), jnp.float32) ** block_scale(key_of[3], (SECTIONS, HEADS), ((0, 16), (1, 64)), -0.2, 0.2), 0.5, 1.5)
    state_in = normal_values(key_of[4], (SECTIONS, GROUPS, SEQLEN, STATE), 1.0, 6.0, ((0, 16), (2, 64)))
    state_out = normal_values(key_of[5], (SECTIONS, GROUPS, SEQLEN, STATE), STATE ** -0.5, 0.5, ((0, 16), (2, 64)))
    segment_ids = jax.vmap(lambda own: jnp.searchsorted(jnp.cumsum(uneven(own, DOCS, SEQLEN, SEQLEN // 2, 2)), jnp.arange(SEQLEN), side="right"))(jax.random.split(key_of[6], SECTIONS)).reshape((SECTIONS, SEQLEN)).astype(jnp.int32)
    return dict(grad_out=grad_out, step_sizes=step_sizes, decay_rate=decay_rate, skip_gain=skip_gain, state_in=state_in, state_out=state_out, segment_ids=segment_ids)


def block_grad(write_block, read_block, seg_block, within_block, total_block, end_block, right_block, grad_block, step_block, skip_local):
    scores = jnp.einsum('ctn,csn->cts', read_block.astype(jnp.float32), write_block.astype(jnp.float32))
    position = jnp.arange(read_block.shape[1])
    causal = position[:, None] >= position[None, :]
    allowed = (seg_block[:, :, None] == seg_block[:, None, :]) & causal[None]
    log_gap = within_block[:, :, :, None] - within_block[:, :, None, :]
    weights = jnp.where(allowed[None], scores[None] * jnp.exp(jnp.where(allowed[None], log_gap, 0.0)), 0.0).astype(jnp.bfloat16)
    within_sum = jnp.einsum('hpct,hcts->hpcs', grad_block.astype(jnp.float32), weights.astype(jnp.float32))
    carried = jnp.einsum('chnp,csn->hpcs', right_block, write_block.astype(jnp.float32), precision=lax.Precision.HIGHEST)
    end_match = (seg_block == end_block[:, None]).astype(jnp.float32)
    carried_sum = carried * (jnp.exp(total_block[:, :, None] - within_block) * end_match[None])[:, None]
    grad_in = step_block[:, None] * (within_sum + carried_sum) + skip_local[:, None, None, None] * grad_block.astype(jnp.float32)
    return grad_in.reshape(grad_block.shape[0] * grad_block.shape[1], -1).astype(jnp.bfloat16)

def group_grad(grad_local, step_local, decay_local, skip_local, write_rows, read_rows, seg_local):
    head_count = step_local.shape[0]
    head_width = grad_local.shape[0] // head_count
    seqlen = write_rows.shape[0]
    span_count = seqlen // SPAN
    width = write_rows.shape[1]
    log_step = -decay_local[:, None] * step_local
    within = jnp.cumsum(log_step.reshape(head_count, span_count, SPAN), axis=2)
    span_total = within[:, :, -1]
    seg_span = seg_local.reshape(span_count, SPAN)
    seg_end = seg_span[:, -1]
    prev_end = jnp.concatenate([seg_end[:1], seg_end[:-1]])
    kept = (seg_span == prev_end[:, None]).astype(jnp.float32)
    read_spans = read_rows.reshape(span_count, SPAN, width)
    write_spans = write_rows.reshape(span_count, SPAN, width)
    read_scaled = (read_spans[None].astype(jnp.float32) * (jnp.exp(within) * kept[None])[..., None]).astype(jnp.bfloat16)
    grad_spans = grad_local.reshape(head_count, head_width, span_count, SPAN)
    local_state = jnp.einsum('hctn,hpct->hcnp', read_scaled.astype(jnp.float32), grad_spans.astype(jnp.float32))
    joined = seg_end == prev_end
    factor = jnp.where(joined[None, :], jnp.exp(span_total), 0.0)

    def recur(state_now, inputs):
        span_state, span_decay = inputs
        return (span_state + span_decay[:, None, None] * state_now, state_now)
    start_state = jnp.zeros((head_count, width, head_width), jnp.float32)
    _, right_state = lax.scan(recur, start_state, (jnp.transpose(local_state, (1, 0, 2, 3)), factor.T), reverse=True)
    step_spans = step_local.reshape(head_count, span_count, SPAN)
    return block_grad(write_spans, read_spans, seg_span, within, span_total, seg_end, right_state, grad_spans, step_spans, skip_local)

def reference(grad_out, step_sizes, decay_rate, skip_gain, state_in, state_out, segment_ids):
    heads_per = HEADS // GROUPS

    def section_grad(inputs):
        grad_local, step_local, decay_local, skip_local, write_all, read_all, seg_local = inputs

        def group_step(group_inputs):
            g_grad, g_step, g_decay, g_skip, g_write, g_read = group_inputs
            return group_grad(g_grad, g_step, g_decay, g_skip, g_write, g_read, seg_local)
        result = lax.map(group_step, (grad_local.reshape(GROUPS, heads_per * HEAD_DIM, SEQLEN), step_local.reshape(GROUPS, heads_per, SEQLEN), decay_local.reshape(GROUPS, heads_per), skip_local.reshape(GROUPS, heads_per), write_all, read_all))
        return result.reshape(HEADS * HEAD_DIM, SEQLEN)
    grad_in = lax.map(section_grad, (grad_out, step_sizes, decay_rate, skip_gain, state_in, state_out, segment_ids))
    return jnp.concatenate([grad_in[1:], jnp.zeros_like(grad_in[:1])], axis=0)
```

```python
import jax
import jax.numpy as jnp
from jax import lax
from jax.experimental import pallas as pl
from jax.experimental.pallas import tpu as pltpu
from jax.sharding import PartitionSpec as P

SPAN = 256
HALF = 128
STATE = 128
SPANS = 32
GROUPS = 8
LEVELS = 4
DOCS = 16
STEP_ROWS = 16
SLAB = 2 * HALF + STEP_ROWS
UNROLL = 4
F32 = jnp.float32
BF16 = jnp.bfloat16


def core_kernel(
    place, decay, skip, seg_ref, grad_ref, *refs
):
    parts, (out_ref, slabs, dt_ref, grow_ref, shrink_ref, carry_ref, keep_ref, fac_ref, end_ref, local_ref, right_ref, sems) = (
        refs[:8],
        refs[8:],
    )
    group, level, core = place[0], place[1], place[2]
    copies = []
    for j in range(LEVELS):
        for other in range(2):
            number = 2 * j + other
            copies.append(
                pltpu.make_async_copy(
                    parts[number], slabs.at[level ^ j, core ^ other], sems.at[number]
                )
            )
    for copy in copies:
        copy.start()

    seg = seg_ref[...]
    last = jnp.broadcast_to(seg[:, SPAN - 1 : SPAN], seg.shape)
    before = jnp.concatenate([last[:1], last[:-1]], axis=0)
    end = jnp.zeros_like(seg)
    for doc in range(DOCS):
        end = jnp.where(seg == doc, jnp.sum((seg <= doc).astype(jnp.int32)), end)
    own = lax.broadcasted_iota(jnp.int32, seg.shape, 0) * SPAN
    end_ref[...] = end - own
    kept = (seg == before).astype(F32)
    at_end = (seg == last).astype(F32)
    joined = (last == before).astype(F32)

    for copy in copies:
        copy.wait()

    def where_is(span):
        source = span // LEVELS
        turned = (source // (GROUPS // 2)) ^ (group // (GROUPS // 2))
        return (span % LEVELS) ^ turned, source

    first_head = 4 * level + 2 * core
    row = lax.broadcasted_iota(jnp.int32, (STEP_ROWS, HALF), 0)

    for span in range(SPANS):
        place_level, source = where_is(span)
        for half in range(2):
            tile = slabs[place_level, half, source, 2 * HALF :, :].astype(F32)
            for head in range(2):
                picked = jnp.sum(
                    jnp.where(row == first_head + head, tile, 0.0), axis=0, keepdims=True
                )
                at = head * SPANS + span
                dt_ref[at : at + 1, half * HALF : (half + 1) * HALF] = picked
    ahead = (
        lax.broadcasted_iota(jnp.int32, (SPAN, SPAN), 0)
        <= lax.broadcasted_iota(jnp.int32, (SPAN, SPAN), 1)
    ).astype(F32).astype(BF16)
    dt = dt_ref[...]
    summed = jnp.dot(dt.astype(BF16), ahead, preferred_element_type=F32)
    for head in range(2):
        rows = slice(head * SPANS, (head + 1) * SPANS)
        within = -decay[head] * summed[rows]
        total = jnp.broadcast_to(within[:, SPAN - 1 : SPAN], within.shape)
        grow = jnp.exp(within)
        grow_ref[rows, :] = grow
        keep_ref[rows, :] = kept
        shrink_ref[rows, :] = dt[rows] * jnp.exp(-within)
        carry_ref[rows, :] = dt[rows] * at_end * jnp.exp(total - within)
        fac_ref[rows, :] = (joined * jnp.exp(total))[:, :STATE]

    def both(ref, span, lanes):
        return jnp.concatenate(
            [
                jnp.broadcast_to(ref[pl.ds(head * SPANS + span, 1), :], (32, lanes))
                for head in range(2)
            ],
            axis=0,
        )

    def grown(span):
        grad = grad_ref[:, pl.ds(pl.multiple_of(span * SPAN, SPAN), SPAN)].astype(F32)
        return grad, (grad * both(grow_ref, span, SPAN))

    def rows_of(span, first):
        place_level, source = where_is(span)
        return jnp.concatenate(
            [slabs[place_level, half, source, first : first + HALF, :] for half in range(2)],
            axis=0,
        )

    def local_of(span, _):
        _, scaled = grown(span)
        masked = (scaled * both(keep_ref, span, SPAN)).astype(BF16)
        local_ref[span] = jnp.dot(masked, rows_of(span, HALF), preferred_element_type=F32)
        return 0

    lax.fori_loop(0, SPANS, local_of, 0, unroll=UNROLL)

    def recur(number, state):
        span = SPANS - 1 - number
        high = state.astype(BF16)
        right_ref[span, 0:64, :] = high
        right_ref[span, 64:128, :] = (state - high.astype(F32)).astype(BF16)
        return local_ref[span] + both(fac_ref, span, STATE) * state

    lax.fori_loop(0, SPANS, recur, jnp.zeros((64, STATE), F32), unroll=UNROLL)
    behind = (
        lax.broadcasted_iota(jnp.int32, (HALF, HALF), 0)
        >= lax.broadcasted_iota(jnp.int32, (HALF, HALF), 1)
    )
    token = lax.broadcasted_iota(jnp.int32, (HALF, HALF), 0)
    gains = jnp.concatenate([jnp.full((32, SPAN), skip[head], F32) for head in range(2)], axis=0)
    nt = (((1,), (1,)), ((), ()))

    def span_of(span, _):
        writes = rows_of(span, 0)
        reads = rows_of(span, HALF)
        grad, scaled = grown(span)
        scaled = scaled.astype(BF16)
        left = jnp.concatenate([reads, right_ref[span]], axis=0)
        product = lax.dot_general(left, writes, nt, preferred_element_type=F32)
        carried = product[SPAN : SPAN + 64] + product[SPAN + 64 :]
        end = end_ref[pl.ds(span, 1), :]
        first_end, second_end = end[:, :HALF], end[:, HALF:]
        s00 = jnp.where(behind & (token < first_end), product[:HALF, :HALF], 0.0).astype(BF16)
        s10 = jnp.where(token + HALF < first_end, product[HALF:SPAN, :HALF], 0.0).astype(BF16)
        s11 = jnp.where(
            behind & (token + HALF < second_end), product[HALF:SPAN, HALF:], 0.0
        ).astype(BF16)
        zero = jnp.zeros((HALF, HALF), BF16)
        scores = jnp.concatenate(
            [jnp.concatenate([s00, zero], axis=1), jnp.concatenate([s10, s11], axis=1)], axis=0
        )
        inner = jnp.dot(scaled, scores, preferred_element_type=F32)
        out = (
            both(shrink_ref, span, SPAN) * inner
            + both(carry_ref, span, SPAN) * carried
            + gains * grad
        )
        out_ref[:, pl.ds(pl.multiple_of(span * SPAN, SPAN), SPAN)] = out.astype(BF16)
        return 0

    lax.fori_loop(0, SPANS, span_of, 0, unroll=UNROLL)


def core_call(place, decay, skip, seg, grad, parts, interpret=False):
    smem = pl.BlockSpec(memory_space=pltpu.SMEM)
    vmem = pl.BlockSpec(memory_space=pltpu.VMEM)
    return pl.pallas_call(
        core_kernel,
        out_shape=jax.ShapeDtypeStruct(grad.shape, BF16),
        in_specs=[smem, smem, smem, vmem, vmem] + [pl.BlockSpec(memory_space=pl.ANY)] * 8,
        out_specs=vmem,
        scratch_shapes=[
            pltpu.VMEM((LEVELS, 2, GROUPS, SLAB, STATE), BF16),
            pltpu.VMEM((2 * SPANS, SPAN), F32),
            pltpu.VMEM((2 * SPANS, SPAN), F32),
            pltpu.VMEM((2 * SPANS, SPAN), F32),
            pltpu.VMEM((2 * SPANS, SPAN), F32),
            pltpu.VMEM((2 * SPANS, SPAN), F32),
            pltpu.VMEM((2 * SPANS, STATE), F32),
            pltpu.VMEM((SPANS, SPAN), jnp.int32),
            pltpu.VMEM((SPANS, 64, STATE), F32),
            pltpu.VMEM((SPANS, 128, STATE), BF16),
            pltpu.SemaphoreType.DMA((8,)),
        ],
        compiler_params=pltpu.CompilerParams(vmem_limit_bytes=24 * 1024 * 1024),
        interpret=interpret,
        name="span_grads",
    )(place, decay, skip, seg, grad, *parts)


def earlier_section(value):
    count = lax.axis_size("section")
    return lax.ppermute(value, "section", [(source, source - 1) for source in range(1, count)])


def level_swap(value, bits):
    return lax.ppermute(value, "seq", [(i, i ^ (2 * bits)) for i in range(64)])


def core_swap(value):
    return lax.ppermute(value, "seq", [(i, i ^ 1) for i in range(64)])


def seq_groups():
    return [
        [8 * g + 2 * (k ^ (g // 4)) + c for g in range(GROUPS)]
        for k in range(LEVELS)
        for c in range(2)
    ]


def local(grad_out, step_sizes, decay_rate, skip_gain, state_in, state_out, segment_ids):
    steps = step_sizes[0].astype(BF16).reshape(GROUPS, STEP_ROWS, HALF)
    slab = jnp.concatenate([state_in[0], state_out[0], steps], axis=1)
    slab = earlier_section(slab)
    grad = earlier_section(grad_out[0])
    seg = earlier_section(segment_ids[0].reshape(SPANS, SPAN))
    params = earlier_section(jnp.stack([decay_rate[0], skip_gain[0]]))
    mine = lax.all_to_all(
        slab, "seq", split_axis=0, concat_axis=0, axis_index_groups=seq_groups(), tiled=True
    )
    parts = []
    for j in range(LEVELS):
        part = level_swap(mine, j) if j else mine
        parts += [part, core_swap(part)]
    seq = lax.axis_index("seq")
    place = jnp.stack([seq // 8, seq // 2 % 4, seq % 2]).astype(jnp.int32)
    out = core_call(place, params[0], params[1], seg, grad, parts)
    return out[None]


def solution(mesh):
    placed = (
        P("section", "seq", None),
        P("section", None, "seq"),
        P("section", "seq"),
        P("section", "seq"),
        P("section", None, "seq", None),
        P("section", None, "seq", None),
        P("section", None),
    )
    return jax.shard_map(
        local, mesh=mesh, in_specs=placed, out_specs=P("section", "seq", None), check_vma=False
    )
```

```python
import functools

import jax
import jax.numpy as jnp
from jax import lax
from jax.experimental import pallas as pl
from jax.experimental.pallas import tpu as pltpu
from jax.sharding import PartitionSpec as P


SPAN = 256
HALF = 128
STATE = 128
SPANS = 32
GROUPS = 8
LEVELS = 4
DOCS = 16
STEP_ROWS = 16
SLAB = 2 * HALF + STEP_ROWS
UNROLL = 4
BASE = (0, 2, 13, 21, 22, 20, 12, 1)
COUNT = (3, 3, 2, 3, 3, 3, 2, 3)
FIRST = (0, 12, 20)
F32 = jnp.float32
BF16 = jnp.bfloat16


def core_kernel(seq, place, small_ref, grad_ref, *refs):
    parts, (out_ref, slabs, dt_ref, grow_ref, shrink_ref, carry_ref, keep_ref, fac_ref, end_ref, local_ref, right_ref, sems) = (
        refs[:6],
        refs[6:],
    )
    seq = lax.axis_index("seq") if seq is None else seq
    group, level, core = seq // 8, (seq // 2) % 4, seq % 2
    copies = []
    for number, part in enumerate(parts):
        copies.append(
            pltpu.make_async_copy(
                part,
                slabs.at[number // 3, pl.ds(FIRST[number % 3], part.shape[0])],
                sems.at[number],
            )
        )
    for copy in copies:
        copy.start()

    seg = small_ref[:SPANS, :].astype(jnp.int32)
    last = jnp.broadcast_to(seg[:, SPAN - 1 : SPAN], seg.shape)
    before = jnp.concatenate([last[:1], last[:-1]], axis=0)
    end = jnp.zeros_like(seg)
    for doc in range(DOCS):
        end = jnp.where(seg == doc, jnp.sum((seg <= doc).astype(jnp.int32)), end)
    own = lax.broadcasted_iota(jnp.int32, seg.shape, 0) * SPAN
    end_ref[...] = end - own
    kept = (seg == before).astype(F32)
    at_end = (seg == last).astype(F32)
    joined = (last == before).astype(F32)

    for copy in copies:
        copy.wait()

    def where_is(span):
        step = (span // LEVELS - group) & (GROUPS - 1)
        return place[step] + ((span % LEVELS) ^ level) * place[GROUPS + step]

    first_head = 4 * level + 2 * core
    row = lax.broadcasted_iota(jnp.int32, (STEP_ROWS, HALF), 0)

    for span in range(SPANS):
        at_slab = where_is(span)
        for half in range(2):
            tile = slabs[half ^ core, at_slab, 2 * HALF :, :].astype(F32)
            for head in range(2):
                picked = jnp.sum(
                    jnp.where(row == first_head + head, tile, 0.0), axis=0, keepdims=True
                )
                at = head * SPANS + span
                dt_ref[at : at + 1, half * HALF : (half + 1) * HALF] = picked
    ahead = (
        lax.broadcasted_iota(jnp.int32, (SPAN, SPAN), 0)
        <= lax.broadcasted_iota(jnp.int32, (SPAN, SPAN), 1)
    ).astype(F32).astype(BF16)
    dt = dt_ref[...]
    summed = jnp.dot(dt.astype(BF16), ahead, preferred_element_type=F32)
    for head in range(2):
        rows = slice(head * SPANS, (head + 1) * SPANS)
        within = -small_ref[SPANS + head : SPANS + head + 1, :] * summed[rows]
        total = jnp.broadcast_to(within[:, SPAN - 1 : SPAN], within.shape)
        grow = jnp.exp(within)
        grow_ref[rows, :] = grow
        keep_ref[rows, :] = kept
        shrink_ref[rows, :] = dt[rows] * jnp.exp(-within)
        carry_ref[rows, :] = dt[rows] * at_end * jnp.exp(total - within)
        fac_ref[rows, :] = (joined * jnp.exp(total))[:, :STATE]

    def both(ref, span, lanes):
        return jnp.concatenate(
            [
                jnp.broadcast_to(ref[pl.ds(head * SPANS + span, 1), :], (32, lanes))
                for head in range(2)
            ],
            axis=0,
        )

    def grown(span):
        grad = grad_ref[:, pl.ds(pl.multiple_of(span * SPAN, SPAN), SPAN)].astype(F32)
        return grad, (grad * both(grow_ref, span, SPAN))

    def rows_of(span, first):
        at_slab = where_is(span)
        return jnp.concatenate(
            [slabs[half ^ core, at_slab, first : first + HALF, :] for half in range(2)],
            axis=0,
        )

    def local_of(span, _):
        _, scaled = grown(span)
        masked = (scaled * both(keep_ref, span, SPAN)).astype(BF16)
        local_ref[span] = jnp.dot(masked, rows_of(span, HALF), preferred_element_type=F32)
        return 0

    lax.fori_loop(0, SPANS, local_of, 0, unroll=UNROLL)

    def recur(number, state):
        span = SPANS - 1 - number
        high = state.astype(BF16)
        right_ref[span, 0:64, :] = high
        right_ref[span, 64:128, :] = (state - high.astype(F32)).astype(BF16)
        return local_ref[span] + both(fac_ref, span, STATE) * state

    lax.fori_loop(0, SPANS, recur, jnp.zeros((64, STATE), F32), unroll=UNROLL)
    behind = (
        lax.broadcasted_iota(jnp.int32, (HALF, HALF), 0)
        >= lax.broadcasted_iota(jnp.int32, (HALF, HALF), 1)
    )
    token = lax.broadcasted_iota(jnp.int32, (HALF, HALF), 0)
    gains = jnp.concatenate(
        [
            jnp.broadcast_to(small_ref[SPANS + 2 + head : SPANS + 3 + head, :], (32, SPAN))
            for head in range(2)
        ],
        axis=0,
    )
    nt = (((1,), (1,)), ((), ()))

    def span_of(span, _):
        writes = rows_of(span, 0)
        reads = rows_of(span, HALF)
        grad, scaled = grown(span)
        scaled = scaled.astype(BF16)
        left = jnp.concatenate([reads, right_ref[span]], axis=0)
        product = lax.dot_general(left, writes, nt, preferred_element_type=F32)
        carried = product[SPAN : SPAN + 64] + product[SPAN + 64 :]
        end = end_ref[pl.ds(span, 1), :]
        first_end, second_end = end[:, :HALF], end[:, HALF:]
        s00 = jnp.where(behind & (token < first_end), product[:HALF, :HALF], 0.0).astype(BF16)
        s10 = jnp.where(token + HALF < first_end, product[HALF:SPAN, :HALF], 0.0).astype(BF16)
        s11 = jnp.where(
            behind & (token + HALF < second_end), product[HALF:SPAN, HALF:], 0.0
        ).astype(BF16)
        zero = jnp.zeros((HALF, HALF), BF16)
        scores = jnp.concatenate(
            [jnp.concatenate([s00, zero], axis=1), jnp.concatenate([s10, s11], axis=1)], axis=0
        )
        inner = jnp.dot(scaled, scores, preferred_element_type=F32)
        out = (
            both(shrink_ref, span, SPAN) * inner
            + both(carry_ref, span, SPAN) * carried
            + gains * grad
        )
        out_ref[:, pl.ds(pl.multiple_of(span * SPAN, SPAN), SPAN)] = out.astype(BF16)
        return 0

    lax.fori_loop(0, SPANS, span_of, 0, unroll=UNROLL)


def core_call(small, grad, parts, seq=None, interpret=False):
    smem = pl.BlockSpec(memory_space=pltpu.SMEM)
    vmem = pl.BlockSpec(memory_space=pltpu.VMEM)
    return pl.pallas_call(
        functools.partial(core_kernel, seq),
        out_shape=jax.ShapeDtypeStruct(grad.shape, BF16),
        in_specs=[smem, vmem, vmem] + [pl.BlockSpec(memory_space=pl.ANY)] * 6,
        out_specs=vmem,
        scratch_shapes=[
            pltpu.VMEM((2, SPANS, SLAB, STATE), BF16),
            pltpu.VMEM((2 * SPANS, SPAN), F32),
            pltpu.VMEM((2 * SPANS, SPAN), F32),
            pltpu.VMEM((2 * SPANS, SPAN), F32),
            pltpu.VMEM((2 * SPANS, SPAN), F32),
            pltpu.VMEM((2 * SPANS, SPAN), F32),
            pltpu.VMEM((2 * SPANS, STATE), F32),
            pltpu.VMEM((SPANS, SPAN), jnp.int32),
            pltpu.VMEM((SPANS, 64, STATE), F32),
            pltpu.VMEM((SPANS, 128, STATE), BF16),
            pltpu.SemaphoreType.DMA((6,)),
        ],
        compiler_params=pltpu.CompilerParams(vmem_limit_bytes=24 * 1024 * 1024),
        interpret=interpret,
        name="span_grads",
    )(jnp.array(BASE + COUNT, jnp.int32), small, grad, *parts)


def shift_pairs(of):
    pairs = []
    for section in range(16):
        for group in range(GROUPS):
            for level in range(LEVELS):
                for core in range(2):
                    target = of(section, group, level, core)
                    if target is not None and target[0] >= 0:
                        there = target[1] % GROUPS * 8 + target[2] * 2 + target[3]
                        pairs.append((section * 64 + group * 8 + level * 2 + core, target[0] * 64 + there))
    return pairs


def moved(value, of):
    return lax.ppermute(value, ("section", "seq"), shift_pairs(of))


def to_group(value, distance):
    return moved(value, lambda s, g, k, c: (s - 1, g + distance, k, c))


def onward(value, distance):
    return moved(value, lambda s, g, k, c: (s, g + distance, k, c))


def levels(value, steps):
    return moved(value, lambda s, g, k, c: (s, g, steps[k], c) if k in steps else None)


def group_gather(chunk, outer):
    middle, ends = {1: 2, 2: 1}, {1: 0, 2: 3}
    near = levels(chunk, {0: 1, 1: 0, 2: 3, 3: 2})
    across = levels(chunk, middle)
    far = levels(near, middle)
    end_near = levels(across, ends)
    end_far = levels(far, ends)
    chunk, near, across, far, end_near, end_far = lax.optimization_barrier(
        (chunk, near, across, far, end_near, end_far)
    )
    every = jnp.concatenate(
        [chunk, near, jnp.where(outer, end_near, far), jnp.where(outer, end_far, across)], axis=0
    )
    other = moved(every, lambda s, g, k, c: (s, g, k, c ^ 1))
    return every.reshape(-1, SLAB, STATE), other.reshape(-1, SLAB, STATE)


def local(grad_out, step_sizes, decay_rate, skip_gain, state_in, state_out, segment_ids):
    seq = lax.axis_index("seq")
    group, level = seq // 8, seq // 2 % 4
    steps = step_sizes[0].astype(BF16).reshape(GROUPS, STEP_ROWS, HALF)
    slab = jnp.concatenate([state_in[0], state_out[0], steps], axis=1)

    def slab_for(distance):
        return lax.dynamic_index_in_dim(slab, (group + distance) % GROUPS, 0, False)

    far = slab_for(4)
    right_1 = to_group(jnp.concatenate([slab_for(1), slab_for(3)]), 1)
    left_1 = to_group(jnp.concatenate([slab_for(7), slab_for(5)]), -1)
    right_2 = to_group(jnp.concatenate([slab_for(2), far[:HALF]]), 2)
    left_2 = to_group(jnp.concatenate([slab_for(6), far[HALF:]]), -2)
    own = to_group(slab_for(0), 0)
    grad = to_group(grad_out[0], 0)
    small = jnp.concatenate(
        [
            segment_ids[0].reshape(SPANS, SPAN).astype(F32),
            jnp.broadcast_to(jnp.concatenate([decay_rate[0], skip_gain[0]])[:, None], (4, SPAN)),
            jnp.zeros((4, SPAN), F32),
        ],
        axis=0,
    )
    small = to_group(small, 0)
    first_in = jnp.concatenate([own, right_1[:SLAB], left_1[:SLAB]])
    right_in = jnp.concatenate([right_1[SLAB:], right_2[SLAB:]])
    left_in = jnp.concatenate([left_1[SLAB:], left_2[SLAB:]])
    second_in = jnp.concatenate([right_2[:SLAB], left_2[:SLAB]])
    right_3 = onward(right_in, 2)
    left_3 = onward(left_in, -2)
    third_in = jnp.concatenate([right_3[:SLAB], left_3[:SLAB], right_3[SLAB:], left_3[SLAB:]])
    outer = (level == 0) | (level == 3)
    first, first_other = group_gather(first_in, outer)
    second, second_other = group_gather(second_in, outer)
    third, third_other = group_gather(third_in, outer)
    out = core_call(
        small, grad, (first, second, third, first_other, second_other, third_other)
    )
    return out[None]


def solution(mesh):
    placed = (
        P("section", "seq", None),
        P("section", None, "seq"),
        P("section", "seq"),
        P("section", "seq"),
        P("section", None, "seq", None),
        P("section", None, "seq", None),
        P("section", None),
    )
    return jax.shard_map(
        local, mesh=mesh, in_specs=placed, out_specs=P("section", "seq", None), check_vma=False
    )
```

```python
import functools

import jax
import jax.numpy as jnp
from jax import lax
from jax.experimental import pallas as pl
from jax.experimental.pallas import tpu as pltpu
from jax.sharding import PartitionSpec as P


SPAN = 256
HALF = 128
STATE = 128
SPANS = 32
GROUPS = 8
LEVELS = 4
DOCS = 16
STEP_ROWS = 16
SLAB = 2 * HALF + STEP_ROWS
UNROLL = 8
BASE = (0, 2, 13, 21, 22, 20, 12, 1)
COUNT = (3, 3, 2, 3, 3, 3, 2, 3)
FIRST = (0, 12, 20)
F32 = jnp.float32
BF16 = jnp.bfloat16


def core_kernel(seq, place, small_ref, grad_ref, *refs):
    parts, (out_ref, slabs, dt_ref, grow_ref, shrink_ref, carry_ref, keep_ref, fac_ref, end_ref, local_ref, right_ref, sems) = (
        refs[:6],
        refs[6:],
    )
    seq = lax.axis_index("seq") if seq is None else seq
    group, level, core = seq // 8, (seq // 2) % 4, seq % 2
    copies = []
    for number, part in enumerate(parts):
        copies.append(
            pltpu.make_async_copy(
                part,
                slabs.at[number // 3, pl.ds(FIRST[number % 3], part.shape[0])],
                sems.at[number],
            )
        )
    for copy in copies:
        copy.start()

    seg = small_ref[:SPANS, :].astype(jnp.int32)
    last = jnp.broadcast_to(seg[:, SPAN - 1 : SPAN], seg.shape)
    before = jnp.concatenate([last[:1], last[:-1]], axis=0)
    end = jnp.zeros_like(seg)
    for doc in range(DOCS):
        end = jnp.where(seg == doc, jnp.sum((seg <= doc).astype(jnp.int32)), end)
    own = lax.broadcasted_iota(jnp.int32, seg.shape, 0) * SPAN
    end_ref[...] = end - own
    kept = (seg == before).astype(F32)
    at_end = (seg == last).astype(F32)
    joined = (last == before).astype(F32)

    for copy in copies:
        copy.wait()

    def where_is(span):
        step = (span // LEVELS - group) & (GROUPS - 1)
        return place[step] + ((span % LEVELS) ^ level) * place[GROUPS + step]

    first_head = 4 * level + 2 * core
    row = lax.broadcasted_iota(jnp.int32, (STEP_ROWS, HALF), 0)

    for span in range(SPANS):
        at_slab = where_is(span)
        for half in range(2):
            tile = slabs[half ^ core, at_slab, 2 * HALF :, :].astype(F32)
            for head in range(2):
                picked = jnp.sum(
                    jnp.where(row == first_head + head, tile, 0.0), axis=0, keepdims=True
                )
                at = head * SPANS + span
                dt_ref[at : at + 1, half * HALF : (half + 1) * HALF] = picked
    ahead = (
        lax.broadcasted_iota(jnp.int32, (SPAN, SPAN), 0)
        <= lax.broadcasted_iota(jnp.int32, (SPAN, SPAN), 1)
    ).astype(F32).astype(BF16)
    dt = dt_ref[...]
    summed = jnp.dot(dt.astype(BF16), ahead, preferred_element_type=F32)
    for head in range(2):
        rows = slice(head * SPANS, (head + 1) * SPANS)
        within = -small_ref[SPANS + head : SPANS + head + 1, :] * summed[rows]
        total = jnp.broadcast_to(within[:, SPAN - 1 : SPAN], within.shape)
        grow = jnp.exp(within)
        grow_ref[rows, :] = grow
        keep_ref[rows, :] = kept
        shrink_ref[rows, :] = dt[rows] * jnp.exp(-within)
        carry_ref[rows, :] = dt[rows] * at_end * jnp.exp(total - within)
        fac_ref[rows, :] = (joined * jnp.exp(total))[:, :STATE]

    def both(ref, span, lanes):
        return jnp.concatenate(
            [
                jnp.broadcast_to(ref[pl.ds(head * SPANS + span, 1), :], (32, lanes))
                for head in range(2)
            ],
            axis=0,
        )

    def grown(span):
        grad = grad_ref[:, pl.ds(pl.multiple_of(span * SPAN, SPAN), SPAN)].astype(F32)
        return grad, (grad * both(grow_ref, span, SPAN))

    def rows_of(span, first):
        at_slab = where_is(span)
        return jnp.concatenate(
            [slabs[half ^ core, at_slab, first : first + HALF, :] for half in range(2)],
            axis=0,
        )

    def locals_of(number, _):
        spans = [number * UNROLL + i for i in range(UNROLL)]
        ready = [
            (
                (grown(span)[1] * both(keep_ref, span, SPAN)).astype(BF16),
                rows_of(span, HALF),
            )
            for span in spans
        ]
        for span, (masked, reads) in zip(spans, ready):
            local_ref[span] = jnp.dot(masked, reads, preferred_element_type=F32)
        return 0

    lax.fori_loop(0, SPANS // UNROLL, locals_of, 0)

    def recur(number, state):
        span = SPANS - 1 - number
        high = state.astype(BF16)
        right_ref[span, 0:64, :] = high
        right_ref[span, 64:128, :] = (state - high.astype(F32)).astype(BF16)
        return local_ref[span] + both(fac_ref, span, STATE) * state

    lax.fori_loop(0, SPANS, recur, jnp.zeros((64, STATE), F32), unroll=UNROLL)
    behind = (
        lax.broadcasted_iota(jnp.int32, (HALF, HALF), 0)
        >= lax.broadcasted_iota(jnp.int32, (HALF, HALF), 1)
    )
    token = lax.broadcasted_iota(jnp.int32, (HALF, HALF), 0)
    gains = jnp.concatenate(
        [
            jnp.broadcast_to(small_ref[SPANS + 2 + head : SPANS + 3 + head, :], (32, SPAN))
            for head in range(2)
        ],
        axis=0,
    )
    nt = (((1,), (1,)), ((), ()))

    def spans_of(number, _):
        spans = [number * UNROLL + i for i in range(UNROLL)]
        left, writes, grads, scaled, ends, shrink, carry = [], [], [], [], [], [], []
        for span in spans:
            writes.append(rows_of(span, 0))
            left.append(jnp.concatenate([rows_of(span, HALF), right_ref[span]], axis=0))
            grad, grow = grown(span)
            grads.append(grad)
            scaled.append(grow.astype(BF16))
            ends.append(end_ref[pl.ds(span, 1), :])
            shrink.append(both(shrink_ref, span, SPAN))
            carry.append(both(carry_ref, span, SPAN))
        outs = []

        def first_of(i):
            return lax.dot_general(left[i], writes[i], nt, preferred_element_type=F32)

        ahead_product = first_of(0)
        for i in range(UNROLL):
            product = ahead_product
            if i + 1 < UNROLL:
                ahead_product = first_of(i + 1)
            carried = product[SPAN : SPAN + 64] + product[SPAN + 64 :]
            first_end, second_end = ends[i][:, :HALF], ends[i][:, HALF:]
            s00 = jnp.where(behind & (token < first_end), product[:HALF, :HALF], 0.0).astype(BF16)
            s10 = jnp.where(token + HALF < first_end, product[HALF:SPAN, :HALF], 0.0).astype(BF16)
            s11 = jnp.where(
                behind & (token + HALF < second_end), product[HALF:SPAN, HALF:], 0.0
            ).astype(BF16)
            zero = jnp.zeros((HALF, HALF), BF16)
            scores = jnp.concatenate(
                [jnp.concatenate([s00, zero], axis=1), jnp.concatenate([s10, s11], axis=1)], axis=0
            )
            inner = jnp.dot(scaled[i], scores, preferred_element_type=F32)
            outs.append((shrink[i] * inner + carry[i] * carried + gains * grads[i]).astype(BF16))
        for i, span in enumerate(spans):
            out_ref[:, pl.ds(pl.multiple_of(span * SPAN, SPAN), SPAN)] = outs[i]
        return 0

    lax.fori_loop(0, SPANS // UNROLL, spans_of, 0)


def core_call(small, grad, parts, seq=None, interpret=False):
    smem = pl.BlockSpec(memory_space=pltpu.SMEM)
    vmem = pl.BlockSpec(memory_space=pltpu.VMEM)
    return pl.pallas_call(
        functools.partial(core_kernel, seq),
        out_shape=jax.ShapeDtypeStruct(grad.shape, BF16),
        in_specs=[smem, vmem, vmem] + [pl.BlockSpec(memory_space=pl.ANY)] * 6,
        out_specs=vmem,
        scratch_shapes=[
            pltpu.VMEM((2, SPANS, SLAB, STATE), BF16),
            pltpu.VMEM((2 * SPANS, SPAN), F32),
            pltpu.VMEM((2 * SPANS, SPAN), F32),
            pltpu.VMEM((2 * SPANS, SPAN), F32),
            pltpu.VMEM((2 * SPANS, SPAN), F32),
            pltpu.VMEM((2 * SPANS, SPAN), F32),
            pltpu.VMEM((2 * SPANS, STATE), F32),
            pltpu.VMEM((SPANS, SPAN), jnp.int32),
            pltpu.VMEM((SPANS, 64, STATE), F32),
            pltpu.VMEM((SPANS, 128, STATE), BF16),
            pltpu.SemaphoreType.DMA((6,)),
        ],
        compiler_params=pltpu.CompilerParams(vmem_limit_bytes=24 * 1024 * 1024),
        interpret=interpret,
        name="span_grads",
    )(jnp.array(BASE + COUNT, jnp.int32), small, grad, *parts)


def shift_pairs(of):
    pairs = []
    for section in range(16):
        for group in range(GROUPS):
            for level in range(LEVELS):
                for core in range(2):
                    target = of(section, group, level, core)
                    if target is not None and target[0] >= 0:
                        there = target[1] % GROUPS * 8 + target[2] * 2 + target[3]
                        pairs.append((section * 64 + group * 8 + level * 2 + core, target[0] * 64 + there))
    return pairs


def moved(value, of):
    return lax.ppermute(value, ("section", "seq"), shift_pairs(of))


def to_group(value, distance):
    return moved(value, lambda s, g, k, c: (s - 1, g + distance, k, c))


def onward(value, distance):
    return moved(value, lambda s, g, k, c: (s, g + distance, k, c))


def levels(value, steps):
    return moved(value, lambda s, g, k, c: (s, g, steps[k], c) if k in steps else None)


def level_gather(chunk):
    chunk = lax.optimization_barrier(chunk)
    others = [moved(chunk, lambda s, g, k, c, j=j: (s, g, k ^ j, c)) for j in (1, 2, 3)]
    every = jnp.concatenate((chunk, *others), axis=0)
    other = moved(every, lambda s, g, k, c: (s, g, k, c ^ 1))
    return every.reshape(-1, SLAB, STATE), other.reshape(-1, SLAB, STATE)


def group_gather(chunk, outer):
    middle, ends = {1: 2, 2: 1}, {1: 0, 2: 3}
    near = levels(chunk, {0: 1, 1: 0, 2: 3, 3: 2})
    across = levels(chunk, middle)
    far = levels(near, middle)
    end_near = levels(across, ends)
    end_far = levels(far, ends)
    chunk, near, across, far, end_near, end_far = lax.optimization_barrier(
        (chunk, near, across, far, end_near, end_far)
    )
    every = jnp.concatenate(
        [chunk, near, jnp.where(outer, end_near, far), jnp.where(outer, end_far, across)],
        axis=0,
    )
    other = moved(every, lambda s, g, k, c: (s, g, k, c ^ 1))
    return every.reshape(-1, SLAB, STATE), other.reshape(-1, SLAB, STATE)


def local(grad_out, step_sizes, decay_rate, skip_gain, state_in, state_out, segment_ids):
    seq = lax.axis_index("seq")
    group, level = seq // 8, seq // 2 % 4
    steps = step_sizes[0].astype(BF16).reshape(GROUPS, STEP_ROWS, HALF)
    slab = jnp.concatenate([state_in[0], state_out[0], steps], axis=1)

    def slab_for(distance):
        return lax.dynamic_index_in_dim(slab, (group + distance) % GROUPS, 0, False)

    far = slab_for(4)
    right_1 = to_group(jnp.concatenate([slab_for(1), slab_for(3)]), 1)
    left_1 = to_group(jnp.concatenate([slab_for(7), slab_for(5)]), -1)
    right_2 = to_group(jnp.concatenate([slab_for(2), far[:HALF]]), 2)
    left_2 = to_group(jnp.concatenate([slab_for(6), far[HALF:]]), -2)
    own = to_group(slab_for(0), 0)
    grad = to_group(grad_out[0], 0)
    small = jnp.concatenate(
        [
            segment_ids[0].reshape(SPANS, SPAN).astype(F32),
            jnp.broadcast_to(jnp.concatenate([decay_rate[0], skip_gain[0]])[:, None], (4, SPAN)),
            jnp.zeros((4, SPAN), F32),
        ],
        axis=0,
    )
    small = to_group(small, 0)
    first_in = jnp.concatenate([own, right_1[:SLAB], left_1[:SLAB]])
    right_in = jnp.concatenate([right_1[SLAB:], right_2[SLAB:]])
    left_in = jnp.concatenate([left_1[SLAB:], left_2[SLAB:]])
    second_in = jnp.concatenate([right_2[:SLAB], left_2[:SLAB]])
    right_3 = onward(right_in, 2)
    left_3 = onward(left_in, -2)
    third_in = jnp.concatenate([right_3[:SLAB], left_3[:SLAB], right_3[SLAB:], left_3[SLAB:]])
    outer = (level == 0) | (level == 3)
    first, first_other = group_gather(first_in, outer)
    second, second_other = level_gather(second_in)
    third, third_other = level_gather(third_in)
    out = core_call(
        small, grad, (first, second, third, first_other, second_other, third_other)
    )
    return out[None]


def solution(mesh):
    placed = (
        P("section", "seq", None),
        P("section", None, "seq"),
        P("section", "seq"),
        P("section", "seq"),
        P("section", None, "seq", None),
        P("section", None, "seq", None),
        P("section", None),
    )
    return jax.shard_map(
        local, mesh=mesh, in_specs=placed, out_specs=P("section", "seq", None), check_vma=False
    )
```
